32 devices in a mesh: tm: 4 (over z), rows: 8 (over y, x, core).
Axes of the slice: x: 2, y: 2, z: 4, core: 2. Of those that a mesh axis runs over, the one named last changes fastest.
Arguments:
- snapshots: float32 [196608, 256], P('rows', 'tm'), may hold values from -100 to 100
- last_snapshot: float32 [196608], P('rows'), may hold values from -100 to 100
Outputs:
- basis_rows: float32 [8, 4, 6144, 256], P('rows', 'tm')
- factor: float32 [256, 256], replicated
- projected: float32 [256, 256], replicated
- operator: float32 [256, 256], replicated
The draws below stay inside these ranges and needn't reach their ends.
All inputs are finite; a program needn't handle non-finite values.
Results may differ from the reference program's by a relative error of at most 0.0003.
Values sent between devices are 32-bit elements; how exact they have to be, the bound alone decides.
No kernel may reach another device: no remote copies, remote signals or barrier semaphores. Data moves between devices by JAX's collectives and lax.ppermute only.
A program may use at most 128 MiB of HBM per device.

```python
import math
import jax
import jax.numpy as jnp
from jax import lax

COLS = 256
RD = 6144
SAMPLES = 196608
N_TM = 4
N_ROWS = 8


def row_traits(key):
    position = jnp.arange(SAMPLES, dtype=jnp.int32)
    rising = jnp.exp(math.log(3.0) * position.astype(jnp.float32) / SAMPLES)[:, None]
    frequency = jax.random.uniform(jax.random.fold_in(key, 21), (SAMPLES, 1), jnp.float32, 0.0, 0.5)
    phase = jax.random.uniform(jax.random.fold_in(key, 22), (SAMPLES, 1), jnp.float32, -math.pi, math.pi)
    amplitude = jax.random.uniform(jax.random.fold_in(key, 23), (SAMPLES, 1), jnp.float32, 3.0, 6.0)
    return (frequency, phase, amplitude, rising)


def draw_snapshots(key, part):
    frequency, phase, amplitude, row_scale = row_traits(key)
    times = jnp.arange(COLS, dtype=jnp.float32)[None, :]
    wave = amplitude * jnp.cos(frequency * times + phase)
    key_noise = jax.random.fold_in(key, 11)
    noise = jax.random.normal(key_noise, (SAMPLES, COLS), jnp.float32)
    position = jnp.arange(SAMPLES, dtype=jnp.int32)
    order = jax.random.permutation(jax.random.fold_in(key, 12), COLS)
    chosen = order[position // RD % COLS]
    columns = jnp.arange(COLS, dtype=jnp.int32)[None, :]
    spike = jnp.where(columns == chosen[:, None], 3.0, 0.0).astype(jnp.float32)
    return jnp.clip((wave + noise + spike) * row_scale, -100.0, 100.0)


def draw_last_snapshot(key, part):
    frequency, phase, amplitude, row_scale = row_traits(key)
    wave = amplitude[:, 0] * jnp.cos(frequency[:, 0] * float(COLS) + phase[:, 0])
    key_noise = jax.random.fold_in(key, 14)
    noise = jax.random.normal(key_noise, (SAMPLES,), jnp.float32)
    return jnp.clip((wave + noise) * row_scale[:, 0], -100.0, 100.0)


def setup_inputs(seed: int = 0) -> dict:
    streams_of = jax.random.split(jax.random.key(seed), 3)
    snapshots = draw_snapshots(jax.random.fold_in(streams_of[2], 71), 0)
    last_snapshot = draw_last_snapshot(jax.random.fold_in(streams_of[2], 71), 0)
    return {"snapshots": snapshots, "last_snapshot": last_snapshot}


def reference(snapshots, last_snapshot):
    highest = lax.Precision.HIGHEST
    samples = snapshots.shape[0]
    gram_matrix = jnp.dot(snapshots.T.astype(jnp.float32), snapshots.astype(jnp.float32), precision=highest, preferred_element_type=jnp.float32) / samples
    tail_column = jnp.dot(last_snapshot.astype(jnp.float32), snapshots.astype(jnp.float32), precision=highest, preferred_element_type=jnp.float32) / samples
    cross_matrix = jnp.concatenate([gram_matrix[:, 1:], tail_column[:, None]], axis=1)
    lower_factor = jnp.linalg.cholesky(gram_matrix)
    identity = jnp.eye(COLS, dtype=jnp.float32)
    inverse = jax.scipy.linalg.solve_triangular(lower_factor, identity, lower=True)
    factor = lower_factor.T
    basis_rows = jnp.dot(snapshots.astype(jnp.float32), inverse.T.astype(jnp.float32), precision=highest, preferred_element_type=jnp.float32)
    projected = jnp.dot(inverse.astype(jnp.float32), cross_matrix.astype(jnp.float32), precision=highest, preferred_element_type=jnp.float32)
    operator = jnp.dot(projected.astype(jnp.float32), inverse.T.astype(jnp.float32), precision=highest, preferred_element_type=jnp.float32)
    return (basis_rows.reshape(N_ROWS, N_TM, RD, COLS), factor, projected, operator)
```

```python
import jax
import jax.numpy as jnp
from jax import lax
from jax.sharding import PartitionSpec as P

AXES = ("tm", "rows")


def sum_all(rows):
    count = lax.axis_size("tm") * lax.axis_size("rows")
    held = rows.shape[0]
    each = -(-held // count)
    padded = jnp.pad(rows, ((0, each * count - held), (0, 0)))
    pieces = lax.all_to_all(padded.reshape(count, each, 128), AXES, 0, 0)
    total = jnp.sum(pieces, axis=0)
    spread = lax.all_to_all(
        jnp.broadcast_to(total[None], (count, each, 128)), AXES, 0, 0
    )
    return spread.reshape(count * each, 128)[:held]


def shards(snapshots, last_snapshot):
    highest = lax.Precision.HIGHEST
    own_cols = snapshots.shape[1]
    tail_own = jnp.dot(
        last_snapshot, snapshots, precision=highest, preferred_element_type=jnp.float32
    )
    local_rows = lax.all_to_all(snapshots, "tm", split_axis=0, concat_axis=1, tiled=True)
    row_count, col_count = local_rows.shape
    half = col_count // 2
    tail_part = lax.dynamic_update_slice_in_dim(
        jnp.zeros((col_count,), jnp.float32), tail_own, lax.axis_index("tm") * own_cols, 0
    )
    gram_part = jnp.dot(
        local_rows.T, local_rows, precision=highest, preferred_element_type=jnp.float32
    )
    samples = row_count * lax.axis_size("tm") * lax.axis_size("rows")
    packed = jnp.concatenate(
        [
            gram_part[:half, :half],
            gram_part[half:, :half],
            gram_part[half:, half:],
            tail_part.reshape(2, half),
        ],
        axis=0,
    )
    total = sum_all(packed) / samples
    low = total[half : 2 * half]
    gram_matrix = jnp.concatenate(
        [
            jnp.concatenate([total[:half], low.T], axis=1),
            jnp.concatenate([low, total[2 * half : 3 * half]], axis=1),
        ],
        axis=0,
    )
    tail_column = total[3 * half :].reshape(col_count)
    cross_matrix = jnp.concatenate([gram_matrix[:, 1:], tail_column[:, None]], axis=1)
    lower_factor = jnp.linalg.cholesky(gram_matrix)
    identity = jnp.eye(col_count, dtype=jnp.float32)
    inverse = jax.scipy.linalg.solve_triangular(lower_factor, identity, lower=True)
    factor = lower_factor.T
    basis_rows = jnp.dot(
        local_rows, inverse.T, precision=highest, preferred_element_type=jnp.float32
    )
    projected = jnp.dot(
        inverse, cross_matrix, precision=highest, preferred_element_type=jnp.float32
    )
    operator = jnp.dot(projected, inverse.T, precision=highest, preferred_element_type=jnp.float32)
    return (basis_rows.reshape(1, 1, row_count, col_count), factor, projected, operator)


def solution(mesh):
    in_specs = (P("rows", "tm"), P("rows"))
    out_specs = (P("rows", "tm", None, None), P(), P(), P())
    return jax.shard_map(shards, mesh=mesh, in_specs=in_specs, out_specs=out_specs, check_vma=False)
```

```python
import functools

import jax
import jax.numpy as jnp
from jax import lax
from jax.experimental import pallas as pl
from jax.experimental.pallas import tpu as pltpu
from jax.sharding import PartitionSpec as P

AXES = ("tm", "rows")
HIGHEST = lax.Precision.HIGHEST
LANES = 128
PANEL = 32
BASIS_TILE = 512
VMEM_LIMIT = 48 * 1024 * 1024


def iota(shape, dim):
    return lax.broadcasted_iota(jnp.int32, shape, dim)


def split(values):
    first = values.astype(jnp.bfloat16)
    second = (values - first.astype(jnp.float32)).astype(jnp.bfloat16)
    return first, second


def dot(left, right, dims=((1,), (0,)), precision=None):
    return lax.dot_general(
        left, right, (dims, ((), ())), precision=precision, preferred_element_type=jnp.float32
    )


def chunk_kernel(*refs, peers, packed_rows):
    pieces = refs[:peers]
    sum_ref, tail_ref, out_ref, high_ref, low_ref, cols_ref = refs[peers:]
    width, depth = pieces[0].shape
    count = width * peers
    me = lax.axis_index("tm")
    for offset, piece in enumerate(pieces):
        start = pl.multiple_of(jnp.bitwise_xor(me, offset) * width, width)
        cols_ref[pl.ds(start, width), :] = piece[...]
    total = None
    step = 2 * LANES if depth % (2 * LANES) == 0 else LANES
    for at in range(0, depth, step):
        cols = cols_ref[:, at : at + step]
        rows = cols.T
        high, low = split(rows)
        high_ref[at : at + step, :] = high
        low_ref[at : at + step, :] = low
        part = dot(cols, rows, precision=HIGHEST)
        total = part if total is None else total + part
    half = count // 2
    blocks = [total[:half, :half], total[:half, half:], total[half:, half:]]
    for index, block in enumerate(blocks):
        at = index * half
        out_ref[at : at + half, :] = sum_ref[at : at + half, :] + block
    pad = jnp.zeros((packed_rows - 3 * half - 8, LANES), jnp.float32)
    out_ref[3 * half : 3 * half + 8, :] = tail_ref[...]
    out_ref[3 * half + 8 :, :] = pad


def add_chunk(pieces, running, tail):
    peers = len(pieces)
    width, depth = pieces[0].shape
    count = width * peers
    packed_rows = running.shape[0]
    vmem = pl.BlockSpec(memory_space=pltpu.VMEM)
    return pl.pallas_call(
        functools.partial(chunk_kernel, peers=peers, packed_rows=packed_rows),
        out_shape=(
            jax.ShapeDtypeStruct((packed_rows, LANES), jnp.float32),
            jax.ShapeDtypeStruct((depth, count), jnp.bfloat16),
            jax.ShapeDtypeStruct((depth, count), jnp.bfloat16),
        ),
        in_specs=[vmem] * (peers + 2),
        out_specs=(vmem,) * 3,
        scratch_shapes=[pltpu.VMEM((count, depth), jnp.float32)],
        compiler_params=pltpu.CompilerParams(vmem_limit_bytes=VMEM_LIMIT),
        cost_estimate=pl.CostEstimate(
            flops=12 * count * count * depth,
            bytes_accessed=8 * count * depth,
            transcendentals=0,
        ),
        name="gram_chunk",
    )(*pieces, running, tail)


def eliminate(rows, at):
    n, count = rows.shape
    sub = iota((n, LANES), 0)
    block = rows[:, at : at + n]
    columns = [jnp.broadcast_to(block[:, k : k + 1], (n, LANES)) for k in range(n)]
    lane, sub_all = iota((n, count), 1), iota((n, count), 0)
    own = (lane >= at) & (lane < at + n)
    rows = jnp.where(own, jnp.where(lane - at == sub_all, 1.0, 0.0), rows)
    halves = [rows[:, h : h + LANES] for h in range(0, count, LANES)]
    pivots = jnp.ones((n, LANES), jnp.float32)
    inverses = jnp.zeros((n, LANES), jnp.float32)
    for k in range(n):
        pivot = columns[k][k : k + 1, :]
        inverse = 1.0 / pivot
        pivots = jnp.where(sub == k, jnp.broadcast_to(pivot, (n, LANES)), pivots)
        inverses = jnp.where(sub == k, jnp.broadcast_to(inverse, (n, LANES)), inverses)
        factor = jnp.where(sub > k, columns[k] * inverse, 0.0)
        for j in range(k + 1, n):
            columns[j] = columns[j] - factor * columns[j][k : k + 1, :]
        halves = [half - factor * half[k : k + 1, :] for half in halves]
    upper = jnp.zeros((n, LANES), jnp.float32)
    lane_here = iota((n, LANES), 1) + at // LANES * LANES
    for k in range(n):
        upper = jnp.where(lane_here == at + k, columns[k], upper)
    return halves, upper, pivots, inverses


def factorize(work, factor_ref, inverse_ref):
    count = work.shape[0]
    n = PANEL
    lane, sub = iota((n, LANES), 1), iota((n, LANES), 0)
    for at in range(0, count, n):
        below = at + n
        halves, upper, pivots, inverses = eliminate(work[at:below, :], at)
        root = lax.rsqrt(pivots)
        root = root * (1.5 - 0.5 * pivots * root * root)
        scaled = []
        for h, half in enumerate(halves):
            column = lane + h * LANES
            mixed = jnp.where((column >= at) & (column < below), upper, half)
            cut = slice(h * LANES, (h + 1) * LANES)
            factor_ref[at:below, cut] = jnp.where(column >= sub + at, mixed * root, 0.0)
            inverse_ref[at:below, cut] = jnp.where(column <= sub + at, half * root, 0.0)
            scaled.append(jnp.where(column >= below, half * inverses, 0.0))
        if below == count:
            break
        skip = below // LANES
        multiplier = jnp.concatenate(scaled[skip:], axis=1)
        update = dot(
            multiplier, jnp.concatenate(halves, axis=1), dims=((0,), (0,)), precision=HIGHEST
        )
        wide = iota((count - below, count), 1)
        old = jnp.where((wide >= at) & (wide < below), 0.0, work[below:, :])
        work[below:, :] = old - update[below - skip * LANES :, :]


def finish_kernel(*refs, chunks, samples):
    total_ref = refs[0]
    high_in, low_in = refs[1 : 1 + chunks], refs[1 + chunks : 1 + 2 * chunks]
    basis_ref, factor_ref, projected_ref, operator_ref = refs[1 + 2 * chunks : 5 + 2 * chunks]
    work, inverse_ref, high_ref, low_ref, rows_ref, in_sem, out_sem = refs[5 + 2 * chunks :]
    count = work.shape[0]
    half = count // 2
    depth = rows_ref.shape[0]

    loads = []
    at = 0
    for index in range(chunks):
        size = high_in[index].shape[0]
        for source, target, lane in ((high_in, high_ref, 0), (low_in, low_ref, 1)):
            copy = pltpu.make_async_copy(
                source[index], target.at[pl.ds(at, size)], in_sem.at[2 * index + lane]
            )
            copy.start()
            loads.append(copy)
        at += size

    scale = 1.0 / samples
    work[:half, :half] = total_ref[:half, :] * scale
    work[:half, half:] = total_ref[half : 2 * half, :] * scale
    work[half:, :half] = jnp.zeros((half, half), jnp.float32)
    work[half:, half:] = total_ref[2 * half : 3 * half, :] * scale
    factorize(work, factor_ref, inverse_ref)

    inverse = inverse_ref[...]
    turned_high, turned_low = split(inverse.T)
    for copy in loads:
        copy.wait()
    stores = []
    for index, at in enumerate(range(0, depth, BASIS_TILE)):
        tile = pl.ds(at, BASIS_TILE)
        high, low = high_ref[tile, :], low_ref[tile, :]
        rows_ref[tile, :] = (
            dot(high, turned_high) + (dot(high, turned_low) + dot(low, turned_high))
        )
        copy = pltpu.make_async_copy(
            rows_ref.at[tile], basis_ref.at[tile], out_sem.at[index]
        )
        copy.start()
        stores.append(copy)

    tail = [total_ref[3 * half + r : 3 * half + r + 1, :] * scale for r in range(2)]
    column = jnp.sum(inverse * jnp.concatenate(tail, axis=1), axis=1, keepdims=True)
    shifted = pltpu.roll(factor_ref[...], count - 1, 1)
    projected = jnp.where(iota((count, count), 1) == count - 1, column, shifted)
    projected_ref[...] = projected
    operator_ref[...] = dot(projected, inverse, dims=((1,), (1,)), precision=HIGHEST)
    for copy in stores:
        copy.wait()


def finish(total, highs, lows, samples):
    chunks = len(highs)
    count = highs[0].shape[1]
    depth = sum(h.shape[0] for h in highs)
    square = jax.ShapeDtypeStruct((count, count), jnp.float32)
    vmem = pl.BlockSpec(memory_space=pltpu.VMEM)
    far = pl.BlockSpec(memory_space=pl.ANY)
    return pl.pallas_call(
        functools.partial(finish_kernel, chunks=chunks, samples=samples),
        out_shape=(jax.ShapeDtypeStruct((depth, count), jnp.float32), square, square, square),
        in_specs=[vmem] + [far] * (2 * chunks),
        out_specs=(far, vmem, vmem, vmem),
        scratch_shapes=[
            pltpu.VMEM((count, count), jnp.float32),
            pltpu.VMEM((count, count), jnp.float32),
            pltpu.VMEM((depth, count), jnp.bfloat16),
            pltpu.VMEM((depth, count), jnp.bfloat16),
            pltpu.VMEM((depth, count), jnp.float32),
            pltpu.SemaphoreType.DMA((2 * chunks,)),
            pltpu.SemaphoreType.DMA((depth // BASIS_TILE,)),
        ],
        compiler_params=pltpu.CompilerParams(vmem_limit_bytes=VMEM_LIMIT),
        name="factor_and_basis",
    )(total, *highs, *lows)


def sum_all(packed):
    devices = lax.axis_size("tm") * lax.axis_size("rows")
    each = packed.shape[0] // devices
    pieces = lax.all_to_all(packed.reshape(devices, each, LANES), AXES, 0, 0)
    total = jnp.sum(pieces, axis=0)
    spread = lax.all_to_all(
        jnp.broadcast_to(total[None], (devices, each, LANES)), AXES, 0, 0
    )
    return spread.reshape(devices * each, LANES)


def shards(snapshots, last_snapshot):
    peers = lax.axis_size("tm")
    devices = peers * lax.axis_size("rows")
    me = lax.axis_index("tm")
    own_cols = snapshots.shape[1]
    count = own_cols * peers
    depth = snapshots.shape[0] // peers
    columns = snapshots.T

    small = depth // 8
    large = (depth - small) // (3 * LANES) * LANES
    sizes = [large, large, depth - small - 2 * large, small]

    chunks = []
    start = 0
    for size in sizes:
        pieces = []
        for offset in range(peers):
            target = jnp.bitwise_xor(me, offset)
            piece = lax.dynamic_slice(columns, (0, target * depth + start), (own_cols, size))
            if offset:
                pairs = [(i, i ^ offset) for i in range(peers)]
                piece = lax.ppermute(piece, "tm", pairs)
            pieces.append(piece)
        chunks.append(pieces)
        start += size

    tail_own = jnp.dot(
        columns, last_snapshot, precision=HIGHEST, preferred_element_type=jnp.float32
    )
    tail = lax.dynamic_update_slice_in_dim(
        jnp.zeros((8 * LANES,), jnp.float32), tail_own, me * own_cols, 0
    ).reshape(8, LANES)

    rows_needed = 3 * (count // 2) + 8
    each = -(-rows_needed // (8 * devices)) * 8
    running = jnp.zeros((each * devices, LANES), jnp.float32)
    highs, lows = [], []
    for pieces in chunks:
        running, high, low = add_chunk(pieces, running, tail)
        highs.append(high)
        lows.append(low)
    total = sum_all(running)
    samples = depth * devices
    basis, factor, projected, operator = finish(total, highs, lows, samples)
    return (basis.reshape(1, 1, depth, count), factor, projected, operator)


def solution(mesh):
    in_specs = (P("rows", "tm"), P("rows"))
    out_specs = (P("rows", "tm", None, None), P(), P(), P())
    return jax.shard_map(shards, mesh=mesh, in_specs=in_specs, out_specs=out_specs, check_vma=False)
```

```python
import functools

import jax
import jax.numpy as jnp
from jax import lax
from jax.experimental import pallas as pl
from jax.experimental.pallas import tpu as pltpu
from jax.sharding import PartitionSpec as P

HIGHEST = lax.Precision.HIGHEST
LANES = 128
PANEL = 32
BASIS_TILE = 512
VMEM_LIMIT = 24 * 1024 * 1024


def iota(shape, dim):
    return lax.broadcasted_iota(jnp.int32, shape, dim)


def split(values):
    first = values.astype(jnp.bfloat16)
    second = (values - first.astype(jnp.float32)).astype(jnp.bfloat16)
    return first, second


def dot(left, right, dims=((1,), (0,)), precision=None):
    return lax.dot_general(
        left, right, (dims, ((), ())), precision=precision, preferred_element_type=jnp.float32
    )


def widen(pieces, cols_ref):
    width = pieces[0].shape[0]
    me = lax.axis_index("tm")
    for offset, piece in enumerate(pieces):
        start = pl.multiple_of(jnp.bitwise_xor(me, offset) * width, width)
        cols_ref[pl.ds(start, width), :] = piece[...]


def gram_of(cols_ref, high_ref, low_ref):
    depth = cols_ref.shape[1]
    total = None
    step = 2 * LANES if depth % (2 * LANES) == 0 else LANES
    for at in range(0, depth, step):
        cols = cols_ref[:, at : at + step]
        rows = cols.T
        high, low = split(rows)
        high_ref[at : at + step, :] = high
        low_ref[at : at + step, :] = low
        part = dot(cols, rows, precision=HIGHEST)
        total = part if total is None else total + part
    half = total.shape[0] // 2
    return total[:half, :half], total[:half, half:], total[half:, half:]


def first_kernel(*refs, peers):
    out_ref, high_ref, low_ref, cols_ref = refs[peers:]
    widen(refs[:peers], cols_ref)
    for index, block in enumerate(gram_of(cols_ref, high_ref, low_ref)):
        out_ref[index] = block


def middle_kernel(*refs, peers):
    sum_ref, out_ref, high_ref, low_ref, cols_ref = refs[peers:]
    widen(refs[:peers], cols_ref)
    for index, block in enumerate(gram_of(cols_ref, high_ref, low_ref)):
        out_ref[index] = sum_ref[index] + block


def last_kernel(*refs, peers):
    sum_ref, tail_ref, keep_ref, send_ref, high_ref, low_ref, cols_ref, pack_ref = refs[peers:]
    widen(refs[:peers], cols_ref)
    first, cross, second = (
        sum_ref[index] + block
        for index, block in enumerate(gram_of(cols_ref, high_ref, low_ref))
    )
    size = first.shape[0]
    row, col = iota(first.shape, 0), iota(first.shape, 1)
    pack_ref[:size, :] = jnp.where(col >= row, first, second)
    pack_ref[size : 2 * size, :] = cross
    pack_ref[2 * size :, :] = jnp.zeros((pack_ref.shape[0] - 2 * size, LANES), jnp.float32)
    pack_ref[2 * size : 2 * size + 1, :] = jnp.sum(
        jnp.where(col == row, second, 0.0), axis=0, keepdims=True
    )
    pack_ref[2 * size + 1 : 2 * size + 3, :] = tail_ref[...]
    rows = keep_ref.shape[0]
    core = jnp.bitwise_and(lax.axis_index("rows"), 1)
    keep_ref[...] = pack_ref[pl.ds(pl.multiple_of(core * rows, 8), rows), :]
    send_ref[...] = pack_ref[pl.ds(pl.multiple_of((1 - core) * rows, 8), rows), :]


def add_chunk(pieces, running, tail):
    peers = len(pieces)
    width, depth = pieces[0].shape
    count = width * peers
    half = count // 2
    vmem = pl.BlockSpec(memory_space=pltpu.VMEM)
    terms = (jax.ShapeDtypeStruct((depth, count), jnp.bfloat16),) * 2
    scratch = [pltpu.VMEM((count, depth), jnp.float32)]
    if tail is None:
        sums = (jax.ShapeDtypeStruct((3, half, half), jnp.float32),)
        args = (*pieces,) if running is None else (*pieces, running)
        body = first_kernel if running is None else middle_kernel
    else:
        rows = (2 * half + 3 + 15) // 16 * 8
        sums = (jax.ShapeDtypeStruct((rows, LANES), jnp.float32),) * 2
        args = (*pieces, running, tail)
        body = last_kernel
        scratch.append(pltpu.VMEM((2 * rows, LANES), jnp.float32))
    return pl.pallas_call(
        functools.partial(body, peers=peers),
        out_shape=sums + terms,
        in_specs=[vmem] * len(args),
        out_specs=(vmem,) * (len(sums) + 2),
        scratch_shapes=scratch,
        compiler_params=pltpu.CompilerParams(vmem_limit_bytes=VMEM_LIMIT),
        cost_estimate=pl.CostEstimate(
            flops=12 * count * count * depth,
            bytes_accessed=8 * count * depth,
            transcendentals=0,
        ),
        name="gram_chunk",
    )(*args)


def eliminate(rows, at):
    n, count = rows.shape
    sub = iota((n, LANES), 0)
    block = rows[:, at : at + n]
    columns = [jnp.broadcast_to(block[:, k : k + 1], (n, LANES)) for k in range(n)]
    lane, sub_all = iota((n, count), 1), iota((n, count), 0)
    own = (lane >= at) & (lane < at + n)
    rows = jnp.where(own, jnp.where(lane - at == sub_all, 1.0, 0.0), rows)
    halves = [rows[:, h : h + LANES] for h in range(0, count, LANES)]
    pivots = jnp.ones((n, LANES), jnp.float32)
    inverses = jnp.zeros((n, LANES), jnp.float32)
    for k in range(n):
        pivot = columns[k][k : k + 1, :]
        inverse = 1.0 / pivot
        pivots = jnp.where(sub == k, jnp.broadcast_to(pivot, (n, LANES)), pivots)
        inverses = jnp.where(sub == k, jnp.broadcast_to(inverse, (n, LANES)), inverses)
        factor = jnp.where(sub > k, columns[k] * inverse, 0.0)
        for j in range(k + 1, n):
            columns[j] = columns[j] - factor * columns[j][k : k + 1, :]
        halves = [half - factor * half[k : k + 1, :] for half in halves]
    upper = jnp.zeros((n, LANES), jnp.float32)
    lane_here = iota((n, LANES), 1) + at // LANES * LANES
    for k in range(n):
        upper = jnp.where(lane_here == at + k, columns[k], upper)
    return halves, upper, pivots, inverses


def factorize(work, factor_ref, inverse_ref):
    count = work.shape[0]
    n = PANEL
    lane, sub = iota((n, LANES), 1), iota((n, LANES), 0)
    for at in range(0, count, n):
        below = at + n
        halves, upper, pivots, inverses = eliminate(work[at:below, :], at)
        root = lax.rsqrt(pivots)
        root = root * (1.5 - 0.5 * pivots * root * root)
        scaled = []
        for h, half in enumerate(halves):
            column = lane + h * LANES
            mixed = jnp.where((column >= at) & (column < below), upper, half)
            cut = slice(h * LANES, (h + 1) * LANES)
            factor_ref[at:below, cut] = jnp.where(column >= sub + at, mixed * root, 0.0)
            inverse_ref[at:below, cut] = jnp.where(column <= sub + at, half * root, 0.0)
            scaled.append(jnp.where(column >= below, half * inverses, 0.0))
        if below == count:
            break
        skip = below // LANES
        multiplier = jnp.concatenate(scaled[skip:], axis=1)
        update = dot(
            multiplier, jnp.concatenate(halves, axis=1), dims=((0,), (0,)), precision=HIGHEST
        )
        wide = iota((count - below, count), 1)
        old = jnp.where((wide >= at) & (wide < below), 0.0, work[below:, :])
        work[below:, :] = old - update[below - skip * LANES :, :]


def finish_kernel(*refs, chunks, samples):
    own_ref, other_ref = refs[:2]
    highs, lows = refs[2 : 2 + chunks], refs[2 + chunks : 2 + 2 * chunks]
    basis_ref, factor_ref, projected_ref, operator_ref = refs[2 + 2 * chunks : 6 + 2 * chunks]
    pack_ref, work, inverse_ref, rows_ref, out_sem = refs[6 + 2 * chunks :]
    count = work.shape[0]
    half = count // 2

    scale = 1.0 / samples
    rows = own_ref.shape[0]
    core = jnp.bitwise_and(lax.axis_index("rows"), 1)
    pack_ref[pl.ds(pl.multiple_of(core * rows, 8), rows), :] = own_ref[...] * scale
    pack_ref[pl.ds(pl.multiple_of((1 - core) * rows, 8), rows), :] = other_ref[...] * scale
    mixed = pack_ref[:half, :]
    row, col = iota((half, half), 0), iota((half, half), 1)
    diagonal = pack_ref[2 * half : 2 * half + 1, :]
    turned = mixed.T
    work[:half, :half] = jnp.where(col >= row, mixed, turned)
    work[:half, half:] = pack_ref[half : 2 * half, :]
    work[half:, :half] = jnp.zeros((half, half), jnp.float32)
    work[half:, half:] = jnp.where(col > row, turned, jnp.where(col == row, diagonal, mixed))
    factorize(work, factor_ref, inverse_ref)

    inverse = inverse_ref[...]
    turned_high, turned_low = split(inverse.T)
    stores = []
    done = 0
    for high_ref, low_ref in zip(highs, lows):
        for at in range(0, high_ref.shape[0], BASIS_TILE):
            size = min(BASIS_TILE, high_ref.shape[0] - at)
            high, low = high_ref[at : at + size, :], low_ref[at : at + size, :]
            tile = pl.ds(done, size)
            rows_ref[tile, :] = (
                dot(high, turned_high) + (dot(high, turned_low) + dot(low, turned_high))
            )
            copy = pltpu.make_async_copy(
                rows_ref.at[tile], basis_ref.at[tile], out_sem.at[len(stores)]
            )
            copy.start()
            stores.append(copy)
            done += size

    tail = [pack_ref[2 * half + r : 2 * half + r + 1, :] for r in (1, 2)]
    column = jnp.sum(inverse * jnp.concatenate(tail, axis=1), axis=1, keepdims=True)
    shifted = pltpu.roll(factor_ref[...], count - 1, 1)
    projected = jnp.where(iota((count, count), 1) == count - 1, column, shifted)
    projected_ref[...] = projected
    operator_ref[...] = dot(projected, inverse, dims=((1,), (1,)), precision=HIGHEST)
    for copy in stores:
        copy.wait()


def finish(own, other, highs, lows, samples):
    chunks = len(highs)
    count = highs[0].shape[1]
    depth = sum(h.shape[0] for h in highs)
    tiles = sum(-(-h.shape[0] // BASIS_TILE) for h in highs)
    square = jax.ShapeDtypeStruct((count, count), jnp.float32)
    vmem = pl.BlockSpec(memory_space=pltpu.VMEM)
    far = pl.BlockSpec(memory_space=pl.ANY)
    return pl.pallas_call(
        functools.partial(finish_kernel, chunks=chunks, samples=samples),
        out_shape=(jax.ShapeDtypeStruct((depth, count), jnp.float32), square, square, square),
        in_specs=[vmem] * (2 + 2 * chunks),
        out_specs=(far, vmem, vmem, vmem),
        scratch_shapes=[
            pltpu.VMEM((2 * own.shape[0], LANES), jnp.float32),
            pltpu.VMEM((count, count), jnp.float32),
            pltpu.VMEM((count, count), jnp.float32),
            pltpu.VMEM((depth, count), jnp.float32),
            pltpu.SemaphoreType.DMA((tiles,)),
        ],
        compiler_params=pltpu.CompilerParams(vmem_limit_bytes=VMEM_LIMIT),
        name="factor_and_basis",
    )(own, other, *highs, *lows)


def swap(values, axis, step):
    size = lax.axis_size(axis)
    return lax.ppermute(values, axis, [(i, i ^ step) for i in range(size)])


def sum_halves(keep, send):
    keep = keep + swap(send, "rows", 1)
    for axis, step in (("rows", 2), ("tm", 1)):
        while step < lax.axis_size(axis):
            keep = keep + swap(keep, axis, step)
            step *= 2
    return keep, swap(keep, "rows", 1)


def shards(snapshots, last_snapshot):
    peers = lax.axis_size("tm")
    devices = peers * lax.axis_size("rows")
    me = lax.axis_index("tm")
    own_cols = snapshots.shape[1]
    count = own_cols * peers
    depth = snapshots.shape[0] // peers
    columns = snapshots.T

    small = depth // 8
    first = depth // 4
    large = (depth - small - first) // (4 * LANES) * (2 * LANES)
    sizes = [first, depth - small - first - large, large, small]

    chunks = []
    start = 0
    for size in sizes:
        pieces = []
        for offset in range(peers):
            target = jnp.bitwise_xor(me, offset)
            pieces.append(
                lax.dynamic_slice(columns, (0, target * depth + start), (own_cols, size))
            )
        if not chunks:
            columns, *pieces = lax.optimization_barrier((columns, *pieces))
            tail_own = jnp.dot(
                columns, last_snapshot, precision=HIGHEST, preferred_element_type=jnp.float32
            )
            columns, tail_own = lax.optimization_barrier((columns, tail_own))
        chunks.append(
            [swap(piece, "tm", offset) if offset else piece for offset, piece in enumerate(pieces)]
        )
        start += size

    tail = lax.dynamic_update_slice_in_dim(
        jnp.zeros((count,), jnp.float32), tail_own, me * own_cols, 0
    ).reshape(count // LANES, LANES)

    running = None
    highs, lows = [], []
    for index, pieces in enumerate(chunks):
        ending = index == len(chunks) - 1
        *running, high, low = add_chunk(pieces, running, tail if ending else None)
        running = running if ending else running[0]
        highs.append(high)
        lows.append(low)
    own, other = sum_halves(*running)
    basis, factor, projected, operator = finish(own, other, highs, lows, depth * devices)
    return (basis.reshape(1, 1, depth, count), factor, projected, operator)


def solution(mesh):
    in_specs = (P("rows", "tm"), P("rows"))
    out_specs = (P("rows", "tm", None, None), P(), P(), P())
    return jax.shard_map(shards, mesh=mesh, in_specs=in_specs, out_specs=out_specs, check_vma=False)
```

```python
import functools

import jax
import jax.numpy as jnp
from jax import lax
from jax.experimental import pallas as pl
from jax.experimental.pallas import tpu as pltpu
from jax.sharding import PartitionSpec as P

HIGHEST = lax.Precision.HIGHEST
LANES = 128
PANEL = 16
BASIS_TILE = 512
VMEM_LIMIT = 24 * 1024 * 1024


def iota(shape, dim):
    return lax.broadcasted_iota(jnp.int32, shape, dim)


def split(values):
    first = values.astype(jnp.bfloat16)
    second = (values - first.astype(jnp.float32)).astype(jnp.bfloat16)
    return first, second


def dot(left, right, dims=((1,), (0,)), precision=None):
    return lax.dot_general(
        left, right, (dims, ((), ())), precision=precision, preferred_element_type=jnp.float32
    )


def widen(pieces, cols_ref):
    width = pieces[0].shape[0]
    me = lax.axis_index("tm")
    for offset, piece in enumerate(pieces):
        start = pl.multiple_of(jnp.bitwise_xor(me, offset) * width, width)
        cols_ref[pl.ds(start, width), :] = piece[...]


def gram_of(cols_ref, high_ref, low_ref):
    depth = cols_ref.shape[1]
    total = None
    step = 2 * LANES if depth % (2 * LANES) == 0 else LANES
    for at in range(0, depth, step):
        cols = cols_ref[:, at : at + step]
        rows = cols.T
        high, low = split(rows)
        high_ref[at : at + step, :] = high
        low_ref[at : at + step, :] = low
        part = dot(cols, rows, precision=HIGHEST)
        total = part if total is None else total + part
    half = total.shape[0] // 2
    return total[:half, :half], total[:half, half:], total[half:, half:]


def first_kernel(*refs, peers):
    out_ref, high_ref, low_ref, cols_ref = refs[peers:]
    widen(refs[:peers], cols_ref)
    for index, block in enumerate(gram_of(cols_ref, high_ref, low_ref)):
        out_ref[index] = block


def middle_kernel(*refs, peers):
    sum_ref, out_ref, high_ref, low_ref, cols_ref = refs[peers:]
    widen(refs[:peers], cols_ref)
    for index, block in enumerate(gram_of(cols_ref, high_ref, low_ref)):
        out_ref[index] = sum_ref[index] + block


def last_kernel(*refs, peers):
    sum_ref, tail_ref, keep_ref, send_ref, high_ref, low_ref, cols_ref, pack_ref = refs[peers:]
    widen(refs[:peers], cols_ref)
    first, cross, second = (
        sum_ref[index] + block
        for index, block in enumerate(gram_of(cols_ref, high_ref, low_ref))
    )
    size = first.shape[0]
    row, col = iota(first.shape, 0), iota(first.shape, 1)
    pack_ref[:size, :] = jnp.where(col >= row, first, second)
    pack_ref[size : 2 * size, :] = cross
    pack_ref[2 * size :, :] = jnp.zeros((pack_ref.shape[0] - 2 * size, LANES), jnp.float32)
    pack_ref[2 * size : 2 * size + 1, :] = jnp.sum(
        jnp.where(col == row, second, 0.0), axis=0, keepdims=True
    )
    pack_ref[2 * size + 1 : 2 * size + 3, :] = tail_ref[...]
    rows = keep_ref.shape[0]
    core = jnp.bitwise_and(lax.axis_index("rows"), 1)
    keep_ref[...] = pack_ref[pl.ds(pl.multiple_of(core * rows, 8), rows), :]
    send_ref[...] = pack_ref[pl.ds(pl.multiple_of((1 - core) * rows, 8), rows), :]


def add_chunk(pieces, running, tail):
    peers = len(pieces)
    width, depth = pieces[0].shape
    count = width * peers
    half = count // 2
    vmem = pl.BlockSpec(memory_space=pltpu.VMEM)
    terms = (jax.ShapeDtypeStruct((depth, count), jnp.bfloat16),) * 2
    scratch = [pltpu.VMEM((count, depth), jnp.float32)]
    if tail is None:
        sums = (jax.ShapeDtypeStruct((3, half, half), jnp.float32),)
        args = (*pieces,) if running is None else (*pieces, running)
        body = first_kernel if running is None else middle_kernel
    else:
        rows = (2 * half + 3 + 15) // 16 * 8
        sums = (jax.ShapeDtypeStruct((rows, LANES), jnp.float32),) * 2
        args = (*pieces, running, tail)
        body = last_kernel
        scratch.append(pltpu.VMEM((2 * rows, LANES), jnp.float32))
    return pl.pallas_call(
        functools.partial(body, peers=peers),
        out_shape=sums + terms,
        in_specs=[vmem] * len(args),
        out_specs=(vmem,) * (len(sums) + 2),
        scratch_shapes=scratch,
        compiler_params=pltpu.CompilerParams(vmem_limit_bytes=VMEM_LIMIT),
        cost_estimate=pl.CostEstimate(
            flops=12 * count * count * depth,
            bytes_accessed=8 * count * depth,
            transcendentals=0,
        ),
        name="gram_chunk",
    )(*args)


def eliminate(rows, following, at):
    n, count = rows.shape
    sub = iota((n, LANES), 0)
    lane, sub_all = iota((n, count), 1), iota((n, count), 0)
    own = (lane >= at) & (lane < at + n)

    def spread(values):
        return [jnp.broadcast_to(values[:, at + k : at + k + 1], (n, LANES)) for k in range(n)]

    def cut(values):
        return [values[:, h : h + LANES] for h in range(0, count, LANES)]

    columns = spread(rows)
    halves = cut(jnp.where(own, jnp.where(lane - at == sub_all, 1.0, 0.0), rows))
    if following is not None:
        next_columns = spread(following)
        next_halves = cut(jnp.where(own, 0.0, following))
    pivots = jnp.ones((n, LANES), jnp.float32)
    inverses = jnp.zeros((n, LANES), jnp.float32)
    for k in range(n):
        pivot = columns[k][k : k + 1, :]
        inverse = 1.0 / pivot
        pivots = jnp.where(sub == k, jnp.broadcast_to(pivot, (n, LANES)), pivots)
        inverses = jnp.where(sub == k, jnp.broadcast_to(inverse, (n, LANES)), inverses)
        factor = jnp.where(sub > k, columns[k] * inverse, 0.0)
        if following is not None:
            next_factor = next_columns[k] * inverse
        for j in range(k + 1, n):
            row = columns[j][k : k + 1, :]
            columns[j] = columns[j] - factor * row
            if following is not None:
                next_columns[j] = next_columns[j] - next_factor * row
        for h, half in enumerate(halves):
            row = half[k : k + 1, :]
            halves[h] = half - factor * row
            if following is not None:
                next_halves[h] = next_halves[h] - next_factor * row
    upper = jnp.zeros((n, LANES), jnp.float32)
    lane_here = iota((n, LANES), 1) + at // LANES * LANES
    for k in range(n):
        upper = jnp.where(lane_here == at + k, columns[k], upper)
    carried = None if following is None else jnp.concatenate(next_halves, axis=1)
    return halves, upper, pivots, inverses, carried


def factorize(work, factor_ref, inverse_ref):
    count = work.shape[0]
    n = PANEL
    lane, sub = iota((n, LANES), 1), iota((n, LANES), 0)
    rows = work[:n, :]
    for at in range(0, count, n):
        below, later = at + n, at + 2 * n
        following = work[below:later, :] if below < count else None
        halves, upper, pivots, inverses, rows = eliminate(rows, following, at)
        root = lax.rsqrt(pivots)
        root = root * (1.5 - 0.5 * pivots * root * root)
        scaled = []
        for h, half in enumerate(halves):
            column = lane + h * LANES
            mixed = jnp.where((column >= at) & (column < below), upper, half)
            cut = slice(h * LANES, (h + 1) * LANES)
            factor_ref[at:below, cut] = jnp.where(column >= sub + at, mixed * root, 0.0)
            inverse_ref[at:below, cut] = jnp.where(column <= sub + at, half * root, 0.0)
            scaled.append(jnp.where(column >= later, half * inverses, 0.0))
        if later >= count:
            continue
        skip = later // LANES
        multiplier = jnp.concatenate(scaled[skip:], axis=1)
        update = dot(
            multiplier, jnp.concatenate(halves, axis=1), dims=((0,), (0,)), precision=HIGHEST
        )
        wide = iota((count - later, count), 1)
        old = jnp.where((wide >= at) & (wide < below), 0.0, work[later:, :])
        work[later:, :] = old - update[later - skip * LANES :, :]


def finish_kernel(*refs, chunks, samples):
    own_ref, other_ref = refs[:2]
    highs, lows = refs[2 : 2 + chunks], refs[2 + chunks : 2 + 2 * chunks]
    basis_ref, factor_ref, projected_ref, operator_ref = refs[2 + 2 * chunks : 6 + 2 * chunks]
    pack_ref, work, inverse_ref, rows_ref, out_sem = refs[6 + 2 * chunks :]
    count = work.shape[0]
    half = count // 2

    scale = 1.0 / samples
    rows = own_ref.shape[0]
    core = jnp.bitwise_and(lax.axis_index("rows"), 1)
    pack_ref[pl.ds(pl.multiple_of(core * rows, 8), rows), :] = own_ref[...] * scale
    pack_ref[pl.ds(pl.multiple_of((1 - core) * rows, 8), rows), :] = other_ref[...] * scale
    mixed = pack_ref[:half, :]
    row, col = iota((half, half), 0), iota((half, half), 1)
    diagonal = pack_ref[2 * half : 2 * half + 1, :]
    turned = mixed.T
    work[:half, :half] = jnp.where(col >= row, mixed, turned)
    cross = pack_ref[half : 2 * half, :]
    work[:half, half:] = cross
    work[half:, :half] = cross.T
    work[half:, half:] = jnp.where(col > row, turned, jnp.where(col == row, diagonal, mixed))
    factorize(work, factor_ref, inverse_ref)

    inverse = inverse_ref[...]
    turned_high, turned_low = split(inverse.T)
    stores = []
    done = 0
    for high_ref, low_ref in zip(highs, lows):
        for at in range(0, high_ref.shape[0], BASIS_TILE):
            size = min(BASIS_TILE, high_ref.shape[0] - at)
            high, low = high_ref[at : at + size, :], low_ref[at : at + size, :]
            tile = pl.ds(done, size)
            rows_ref[tile, :] = (
                dot(high, turned_high) + (dot(high, turned_low) + dot(low, turned_high))
            )
            copy = pltpu.make_async_copy(
                rows_ref.at[tile], basis_ref.at[tile], out_sem.at[len(stores)]
            )
            copy.start()
            stores.append(copy)
            done += size

    tail = [pack_ref[2 * half + r : 2 * half + r + 1, :] for r in (1, 2)]
    column = jnp.sum(inverse * jnp.concatenate(tail, axis=1), axis=1, keepdims=True)
    shifted = pltpu.roll(factor_ref[...], count - 1, 1)
    projected = jnp.where(iota((count, count), 1) == count - 1, column, shifted)
    projected_ref[...] = projected
    operator_ref[...] = dot(projected, inverse, dims=((1,), (1,)), precision=HIGHEST)
    for copy in stores:
        copy.wait()


def finish(own, other, highs, lows, samples):
    chunks = len(highs)
    count = highs[0].shape[1]
    depth = sum(h.shape[0] for h in highs)
    tiles = sum(-(-h.shape[0] // BASIS_TILE) for h in highs)
    square = jax.ShapeDtypeStruct((count, count), jnp.float32)
    vmem = pl.BlockSpec(memory_space=pltpu.VMEM)
    far = pl.BlockSpec(memory_space=pl.ANY)
    return pl.pallas_call(
        functools.partial(finish_kernel, chunks=chunks, samples=samples),
        out_shape=(jax.ShapeDtypeStruct((depth, count), jnp.float32), square, square, square),
        in_specs=[vmem] * (2 + 2 * chunks),
        out_specs=(far, vmem, vmem, vmem),
        scratch_shapes=[
            pltpu.VMEM((2 * own.shape[0], LANES), jnp.float32),
            pltpu.VMEM((count, count), jnp.float32),
            pltpu.VMEM((count, count), jnp.float32),
            pltpu.VMEM((depth, count), jnp.float32),
            pltpu.SemaphoreType.DMA((tiles,)),
        ],
        compiler_params=pltpu.CompilerParams(vmem_limit_bytes=VMEM_LIMIT),
        name="factor_and_basis",
    )(own, other, *highs, *lows)


def swap(values, axis, step):
    size = lax.axis_size(axis)
    return lax.ppermute(values, axis, [(i, i ^ step) for i in range(size)])


def sum_halves(keep, send):
    keep = keep + swap(send, "rows", 1)
    for axis, step in (("rows", 2), ("tm", 1)):
        while step < lax.axis_size(axis):
            keep = keep + swap(keep, axis, step)
            step *= 2
    return keep, swap(keep, "rows", 1)


def shards(snapshots, last_snapshot):
    peers = lax.axis_size("tm")
    devices = peers * lax.axis_size("rows")
    me = lax.axis_index("tm")
    own_cols = snapshots.shape[1]
    count = own_cols * peers
    depth = snapshots.shape[0] // peers
    columns = snapshots.T

    small = depth // 8
    first = depth // 6 // LANES * LANES
    large = (depth - small - first) // (4 * LANES) * (2 * LANES)
    sizes = [first, depth - small - first - large, large, small]

    def cut(values, offset, start, size):
        target = jnp.bitwise_xor(me, offset)
        return lax.dynamic_slice(values, (0, target * depth + start), (own_cols, size))

    far = range(2, peers)
    columns, *early = lax.optimization_barrier(
        (columns, *[cut(columns, offset, 0, first) for offset in far])
    )
    early = {offset: swap(piece, "tm", offset) for offset, piece in zip(far, early)}
    tail_own = jnp.dot(
        columns, last_snapshot, precision=HIGHEST, preferred_element_type=jnp.float32
    )
    columns, tail_own = lax.optimization_barrier((columns, tail_own))
    chunks = []
    start = 0
    for size in sizes:
        pieces = []
        for offset in range(peers):
            if start == 0 and offset in early:
                pieces.append(early[offset])
                continue
            piece = cut(columns, offset, start, size)
            pieces.append(swap(piece, "tm", offset) if offset else piece)
        chunks.append(pieces)
        start += size

    tail = lax.dynamic_update_slice_in_dim(
        jnp.zeros((count,), jnp.float32), tail_own, me * own_cols, 0
    ).reshape(count // LANES, LANES)

    running = None
    highs, lows = [], []
    for index, pieces in enumerate(chunks):
        ending = index == len(chunks) - 1
        *running, high, low = add_chunk(pieces, running, tail if ending else None)
        running = running if ending else running[0]
        highs.append(high)
        lows.append(low)
    own, other = sum_halves(*running)
    basis, factor, projected, operator = finish(own, other, highs, lows, depth * devices)
    return (basis.reshape(1, 1, depth, count), factor, projected, operator)


def solution(mesh):
    in_specs = (P("rows", "tm"), P("rows"))
    out_specs = (P("rows", "tm", None, None), P(), P(), P())
    return jax.shard_map(shards, mesh=mesh, in_specs=in_specs, out_specs=out_specs, check_vma=False)
```

```python
import functools

import jax
import jax.numpy as jnp
from jax import lax
from jax.experimental import pallas as pl
from jax.experimental.pallas import tpu as pltpu
from jax.sharding import PartitionSpec as P

HIGHEST = lax.Precision.HIGHEST
LANES = 128
PANEL = 16
BASIS_TILE = 512
VMEM_LIMIT = 24 * 1024 * 1024


def iota(shape, dim):
    return lax.broadcasted_iota(jnp.int32, shape, dim)


def split(values):
    first = values.astype(jnp.bfloat16)
    second = (values - first.astype(jnp.float32)).astype(jnp.bfloat16)
    return first, second


def dot(left, right, dims=((1,), (0,)), precision=None):
    return lax.dot_general(
        left, right, (dims, ((), ())), precision=precision, preferred_element_type=jnp.float32
    )


def widen(pieces, cols_ref):
    width = pieces[0].shape[0]
    me = lax.axis_index("tm")
    for offset, piece in enumerate(pieces):
        start = pl.multiple_of(jnp.bitwise_xor(me, offset) * width, width)
        cols_ref[pl.ds(start, width), :] = piece[...]


def gram_of(cols_ref, high_ref, low_ref):
    depth = cols_ref.shape[1]
    total = None
    step = 2 * LANES if depth % (2 * LANES) == 0 else LANES
    for at in range(0, depth, step):
        cols = cols_ref[:, at : at + step]
        rows = cols.T
        high, low = split(rows)
        high_ref[at : at + step, :] = high
        low_ref[at : at + step, :] = low
        part = dot(cols, rows, precision=HIGHEST)
        total = part if total is None else total + part
    half = total.shape[0] // 2
    return total[:half, :half], total[:half, half:], total[half:, half:]


def first_kernel(*refs, peers):
    out_ref, high_ref, low_ref, cols_ref = refs[peers:]
    widen(refs[:peers], cols_ref)
    for index, block in enumerate(gram_of(cols_ref, high_ref, low_ref)):
        out_ref[index] = block


def middle_kernel(*refs, peers):
    sum_ref, out_ref, high_ref, low_ref, cols_ref = refs[peers:]
    widen(refs[:peers], cols_ref)
    for index, block in enumerate(gram_of(cols_ref, high_ref, low_ref)):
        out_ref[index] = sum_ref[index] + block


def last_kernel(*refs, peers):
    sum_ref, tail_ref, keep_ref, send_ref, high_ref, low_ref, cols_ref, pack_ref = refs[peers:]
    widen(refs[:peers], cols_ref)
    first, cross, second = (
        sum_ref[index] + block
        for index, block in enumerate(gram_of(cols_ref, high_ref, low_ref))
    )
    size = first.shape[0]
    row, col = iota(first.shape, 0), iota(first.shape, 1)
    pack_ref[:size, :] = jnp.where(col >= row, first, second)
    pack_ref[size : 2 * size, :] = cross
    pack_ref[2 * size :, :] = jnp.zeros((pack_ref.shape[0] - 2 * size, LANES), jnp.float32)
    pack_ref[2 * size : 2 * size + 1, :] = jnp.sum(
        jnp.where(col == row, second, 0.0), axis=0, keepdims=True
    )
    pack_ref[2 * size + 1 : 2 * size + 3, :] = tail_ref[...]
    rows = keep_ref.shape[0]
    core = jnp.bitwise_and(lax.axis_index("rows"), 1)
    keep_ref[...] = pack_ref[pl.ds(pl.multiple_of(core * rows, 8), rows), :]
    send_ref[...] = pack_ref[pl.ds(pl.multiple_of((1 - core) * rows, 8), rows), :]


def add_chunk(pieces, running, tail):
    peers = len(pieces)
    width, depth = pieces[0].shape
    count = width * peers
    half = count // 2
    vmem = pl.BlockSpec(memory_space=pltpu.VMEM)
    terms = (jax.ShapeDtypeStruct((depth, count), jnp.bfloat16),) * 2
    scratch = [pltpu.VMEM((count, depth), jnp.float32)]
    if tail is None:
        sums = (jax.ShapeDtypeStruct((3, half, half), jnp.float32),)
        args = (*pieces,) if running is None else (*pieces, running)
        body = first_kernel if running is None else middle_kernel
    else:
        rows = (2 * half + 3 + 15) // 16 * 8
        sums = (jax.ShapeDtypeStruct((rows, LANES), jnp.float32),) * 2
        args = (*pieces, running, tail)
        body = last_kernel
        scratch.append(pltpu.VMEM((2 * rows, LANES), jnp.float32))
    return pl.pallas_call(
        functools.partial(body, peers=peers),
        out_shape=sums + terms,
        in_specs=[vmem] * len(args),
        out_specs=(vmem,) * (len(sums) + 2),
        scratch_shapes=scratch,
        compiler_params=pltpu.CompilerParams(vmem_limit_bytes=VMEM_LIMIT),
        cost_estimate=pl.CostEstimate(
            flops=12 * count * count * depth,
            bytes_accessed=8 * count * depth,
            transcendentals=0,
        ),
        name="gram_chunk",
    )(*args)


def eliminate(rows, following, at):
    n, count = rows.shape
    sub = iota((n, LANES), 0)
    lane, sub_all = iota((n, count), 1), iota((n, count), 0)
    own = (lane >= at) & (lane < at + n)

    def spread(values):
        return [jnp.broadcast_to(values[:, at + k : at + k + 1], (n, LANES)) for k in range(n)]

    def cut(values):
        return [values[:, h : h + LANES] for h in range(0, count, LANES)]

    columns = spread(rows)
    halves = cut(jnp.where(own, jnp.where(lane - at == sub_all, 1.0, 0.0), rows))
    if following is not None:
        next_columns = spread(following)
        next_halves = cut(jnp.where(own, 0.0, following))
    pivots = jnp.ones((n, LANES), jnp.float32)
    inverses = jnp.zeros((n, LANES), jnp.float32)
    for k in range(n):
        pivot = columns[k][k : k + 1, :]
        inverse = 1.0 / pivot
        pivots = jnp.where(sub == k, jnp.broadcast_to(pivot, (n, LANES)), pivots)
        inverses = jnp.where(sub == k, jnp.broadcast_to(inverse, (n, LANES)), inverses)
        factor = jnp.where(sub > k, columns[k] * inverse, 0.0)
        if following is not None:
            next_factor = next_columns[k] * inverse
        for j in range(k + 1, n):
            row = columns[j][k : k + 1, :]
            columns[j] = columns[j] - factor * row
            if following is not None:
                next_columns[j] = next_columns[j] - next_factor * row
        for h, half in enumerate(halves):
            row = half[k : k + 1, :]
            halves[h] = half - factor * row
            if following is not None:
                next_halves[h] = next_halves[h] - next_factor * row
    upper = jnp.zeros((n, LANES), jnp.float32)
    lane_here = iota((n, LANES), 1) + at // LANES * LANES
    for k in range(n):
        upper = jnp.where(lane_here == at + k, columns[k], upper)
    carried = None if following is None else jnp.concatenate(next_halves, axis=1)
    return halves, upper, pivots, inverses, carried


def factorize(work, factor_ref, inverse_ref):
    count = work.shape[0]
    n = PANEL
    lane, sub = iota((n, LANES), 1), iota((n, LANES), 0)
    rows = work[:n, :]
    for at in range(0, count, n):
        below, later = at + n, at + 2 * n
        following = work[below:later, :] if below < count else None
        halves, upper, pivots, inverses, rows = eliminate(rows, following, at)
        root = lax.rsqrt(pivots)
        root = root * (1.5 - 0.5 * pivots * root * root)
        scaled = []
        for h, half in enumerate(halves):
            column = lane + h * LANES
            mixed = jnp.where((column >= at) & (column < below), upper, half)
            cut = slice(h * LANES, (h + 1) * LANES)
            factor_ref[at:below, cut] = jnp.where(column >= sub + at, mixed * root, 0.0)
            inverse_ref[at:below, cut] = jnp.where(column <= sub + at, half * root, 0.0)
            scaled.append(jnp.where(column >= later, half * inverses, 0.0))
        if later >= count:
            continue
        skip = later // LANES
        multiplier = jnp.concatenate([part.T for part in scaled[skip:]], axis=0)
        finished = jnp.concatenate(halves, axis=1)
        for top, end in ((later, later + n), (later + n, count)):
            if top >= end:
                continue
            from_row = skip * LANES
            update = dot(multiplier[top - from_row : end - from_row], finished, precision=HIGHEST)
            wide = iota((end - top, count), 1)
            old = jnp.where((wide >= at) & (wide < below), 0.0, work[top:end, :])
            work[top:end, :] = old - update


def finish_kernel(*refs, chunks, samples):
    own_ref, other_ref = refs[:2]
    highs, lows = refs[2 : 2 + chunks], refs[2 + chunks : 2 + 2 * chunks]
    basis_ref, factor_ref, projected_ref, operator_ref = refs[2 + 2 * chunks : 6 + 2 * chunks]
    pack_ref, work, inverse_ref, rows_ref, out_sem = refs[6 + 2 * chunks :]
    count = work.shape[0]
    half = count // 2

    scale = 1.0 / samples
    rows = own_ref.shape[0]
    core = jnp.bitwise_and(lax.axis_index("rows"), 1)
    pack_ref[pl.ds(pl.multiple_of(core * rows, 8), rows), :] = own_ref[...] * scale
    pack_ref[pl.ds(pl.multiple_of((1 - core) * rows, 8), rows), :] = other_ref[...] * scale
    mixed = pack_ref[:half, :]
    row, col = iota((half, half), 0), iota((half, half), 1)
    diagonal = pack_ref[2 * half : 2 * half + 1, :]
    turned = mixed.T
    work[:half, :half] = jnp.where(col >= row, mixed, turned)
    cross = pack_ref[half : 2 * half, :]
    work[:half, half:] = cross
    work[half:, :half] = cross.T
    work[half:, half:] = jnp.where(col > row, turned, jnp.where(col == row, diagonal, mixed))
    factorize(work, factor_ref, inverse_ref)

    inverse = inverse_ref[...]
    turned_high, turned_low = split(inverse.T)
    stores = []
    done = 0
    for high_ref, low_ref in zip(highs, lows):
        for at in range(0, high_ref.shape[0], BASIS_TILE):
            size = min(BASIS_TILE, high_ref.shape[0] - at)
            high, low = high_ref[at : at + size, :], low_ref[at : at + size, :]
            tile = pl.ds(done, size)
            rows_ref[tile, :] = (
                dot(high, turned_high) + (dot(high, turned_low) + dot(low, turned_high))
            )
            copy = pltpu.make_async_copy(
                rows_ref.at[tile], basis_ref.at[tile], out_sem.at[len(stores)]
            )
            copy.start()
            stores.append(copy)
            done += size

    tail = [pack_ref[2 * half + r : 2 * half + r + 1, :] for r in (1, 2)]
    column = jnp.sum(inverse * jnp.concatenate(tail, axis=1), axis=1, keepdims=True)
    shifted = pltpu.roll(factor_ref[...], count - 1, 1)
    projected = jnp.where(iota((count, count), 1) == count - 1, column, shifted)
    projected_ref[...] = projected
    operator_ref[...] = dot(projected, inverse, dims=((1,), (1,)), precision=HIGHEST)
    for copy in stores:
        copy.wait()


def finish(own, other, highs, lows, samples):
    chunks = len(highs)
    count = highs[0].shape[1]
    depth = sum(h.shape[0] for h in highs)
    tiles = sum(-(-h.shape[0] // BASIS_TILE) for h in highs)
    square = jax.ShapeDtypeStruct((count, count), jnp.float32)
    vmem = pl.BlockSpec(memory_space=pltpu.VMEM)
    far = pl.BlockSpec(memory_space=pl.ANY)
    return pl.pallas_call(
        functools.partial(finish_kernel, chunks=chunks, samples=samples),
        out_shape=(jax.ShapeDtypeStruct((depth, count), jnp.float32), square, square, square),
        in_specs=[vmem] * (2 + 2 * chunks),
        out_specs=(far, vmem, vmem, vmem),
        scratch_shapes=[
            pltpu.VMEM((2 * own.shape[0], LANES), jnp.float32),
            pltpu.VMEM((count, count), jnp.float32),
            pltpu.VMEM((count, count), jnp.float32),
            pltpu.VMEM((depth, count), jnp.float32),
            pltpu.SemaphoreType.DMA((tiles,)),
        ],
        compiler_params=pltpu.CompilerParams(vmem_limit_bytes=VMEM_LIMIT),
        name="factor_and_basis",
    )(own, other, *highs, *lows)


def swap(values, axis, step):
    size = lax.axis_size(axis)
    return lax.ppermute(values, axis, [(i, i ^ step) for i in range(size)])


def sum_halves(keep, send):
    keep = keep + swap(send, "rows", 1)
    for axis, step in (("rows", 2), ("tm", 1)):
        size = lax.axis_size(axis)
        while step < size:
            if 2 * step < size:
                far = swap(keep, axis, 3 * step)
                near = swap(keep, axis, step)
                other = swap(keep, axis, 2 * step)
                keep = (keep + near) + (other + far)
            else:
                keep = keep + swap(keep, axis, step)
            step *= 4
    return keep, swap(keep, "rows", 1)


def shards(snapshots, last_snapshot):
    peers = lax.axis_size("tm")
    devices = peers * lax.axis_size("rows")
    me = lax.axis_index("tm")
    own_cols = snapshots.shape[1]
    count = own_cols * peers
    depth = snapshots.shape[0] // peers
    columns = snapshots.T

    small = depth // 8
    first = depth // 6 // LANES * LANES
    large = (depth - small - first) // (4 * LANES) * (2 * LANES)
    sizes = [first, depth - small - first - large, large, small]

    def cut(values, offset, start, size):
        target = jnp.bitwise_xor(me, offset)
        return lax.dynamic_slice(values, (0, target * depth + start), (own_cols, size))

    far = range(2, peers)
    columns, *early = lax.optimization_barrier(
        (columns, *[cut(columns, offset, 0, first) for offset in far])
    )
    early = {offset: swap(piece, "tm", offset) for offset, piece in zip(far, early)}
    tail_own = jnp.dot(
        columns, last_snapshot, precision=HIGHEST, preferred_element_type=jnp.float32
    )
    columns, tail_own = lax.optimization_barrier((columns, tail_own))
    chunks = []
    start = 0
    for size in sizes:
        pieces = []
        for offset in range(peers):
            if start == 0 and offset in early:
                pieces.append(early[offset])
                continue
            piece = cut(columns, offset, start, size)
            pieces.append(swap(piece, "tm", offset) if offset else piece)
        chunks.append(pieces)
        start += size

    tail = lax.dynamic_update_slice_in_dim(
        jnp.zeros((count,), jnp.float32), tail_own, me * own_cols, 0
    ).reshape(count // LANES, LANES)

    running = None
    highs, lows = [], []
    for index, pieces in enumerate(chunks):
        ending = index == len(chunks) - 1
        *running, high, low = add_chunk(pieces, running, tail if ending else None)
        running = running if ending else running[0]
        highs.append(high)
        lows.append(low)
    own, other = sum_halves(*running)
    basis, factor, projected, operator = finish(own, other, highs, lows, depth * devices)
    return (basis.reshape(1, 1, depth, count), factor, projected, operator)


def solution(mesh):
    in_specs = (P("rows", "tm"), P("rows"))
    out_specs = (P("rows", "tm", None, None), P(), P(), P())
    return jax.shard_map(shards, mesh=mesh, in_specs=in_specs, out_specs=out_specs, check_vma=False)
```

```python
import functools

import jax
import jax.numpy as jnp
from jax import lax
from jax.experimental import pallas as pl
from jax.experimental.pallas import tpu as pltpu
from jax.sharding import PartitionSpec as P

HIGHEST = lax.Precision.HIGHEST
LANES = 128
PANEL = 16
BASIS_TILE = 256
VMEM_LIMIT = 24 * 1024 * 1024


def iota(shape, dim):
    return lax.broadcasted_iota(jnp.int32, shape, dim)


def split(values):
    first = values.astype(jnp.bfloat16)
    second = (values - first.astype(jnp.float32)).astype(jnp.bfloat16)
    return first, second


def dot(left, right, dims=((1,), (0,)), precision=None):
    return lax.dot_general(
        left, right, (dims, ((), ())), precision=precision, preferred_element_type=jnp.float32
    )


def widen(pieces, cols_ref):
    width = pieces[0].shape[0]
    me = lax.axis_index("tm")
    for offset, piece in enumerate(pieces):
        start = pl.multiple_of(jnp.bitwise_xor(me, offset) * width, width)
        cols_ref[pl.ds(start, width), :] = piece[...]


def gram_of(cols_ref, high_ref, low_ref):
    depth = cols_ref.shape[1]
    total = None
    step = 2 * LANES if depth % (2 * LANES) == 0 else LANES
    for at in range(0, depth, step):
        cols = cols_ref[:, at : at + step]
        rows = cols.T
        high, low = split(rows)
        high_ref[at : at + step, :] = high
        low_ref[at : at + step, :] = low
        part = dot(cols, rows, precision=HIGHEST)
        total = part if total is None else total + part
    half = total.shape[0] // 2
    return total[:half, :half], total[:half, half:], total[half:, half:]


def first_kernel(*refs, peers):
    out_ref, high_ref, low_ref, cols_ref = refs[peers:]
    widen(refs[:peers], cols_ref)
    for index, block in enumerate(gram_of(cols_ref, high_ref, low_ref)):
        out_ref[index] = block


def middle_kernel(*refs, peers):
    sum_ref, out_ref, high_ref, low_ref, cols_ref = refs[peers:]
    widen(refs[:peers], cols_ref)
    for index, block in enumerate(gram_of(cols_ref, high_ref, low_ref)):
        out_ref[index] = sum_ref[index] + block


def last_kernel(*refs, peers):
    sum_ref, tail_ref, keep_ref, send_ref, high_ref, low_ref, cols_ref, pack_ref = refs[peers:]
    widen(refs[:peers], cols_ref)
    first, cross, second = (
        sum_ref[index] + block
        for index, block in enumerate(gram_of(cols_ref, high_ref, low_ref))
    )
    size = first.shape[0]
    row, col = iota(first.shape, 0), iota(first.shape, 1)
    pack_ref[:size, :] = jnp.where(col >= row, first, second)
    pack_ref[size : 2 * size, :] = cross
    pack_ref[2 * size :, :] = jnp.zeros((pack_ref.shape[0] - 2 * size, LANES), jnp.float32)
    pack_ref[2 * size : 2 * size + 1, :] = jnp.sum(
        jnp.where(col == row, second, 0.0), axis=0, keepdims=True
    )
    pack_ref[2 * size + 1 : 2 * size + 3, :] = tail_ref[...]
    rows = keep_ref.shape[0]
    core = jnp.bitwise_and(lax.axis_index("rows"), 1)
    keep_ref[...] = pack_ref[pl.ds(pl.multiple_of(core * rows, 8), rows), :]
    send_ref[...] = pack_ref[pl.ds(pl.multiple_of((1 - core) * rows, 8), rows), :]


def add_chunk(pieces, running, tail):
    peers = len(pieces)
    width, depth = pieces[0].shape
    count = width * peers
    half = count // 2
    vmem = pl.BlockSpec(memory_space=pltpu.VMEM)
    terms = (jax.ShapeDtypeStruct((depth, count), jnp.bfloat16),) * 2
    scratch = [pltpu.VMEM((count, depth), jnp.float32)]
    if tail is None:
        sums = (jax.ShapeDtypeStruct((3, half, half), jnp.float32),)
        args = (*pieces,) if running is None else (*pieces, running)
        body = first_kernel if running is None else middle_kernel
    else:
        rows = (2 * half + 3 + 15) // 16 * 8
        sums = (jax.ShapeDtypeStruct((rows, LANES), jnp.float32),) * 2
        args = (*pieces, running, tail)
        body = last_kernel
        scratch.append(pltpu.VMEM((2 * rows, LANES), jnp.float32))
    return pl.pallas_call(
        functools.partial(body, peers=peers),
        out_shape=sums + terms,
        in_specs=[vmem] * len(args),
        out_specs=(vmem,) * (len(sums) + 2),
        scratch_shapes=scratch,
        compiler_params=pltpu.CompilerParams(vmem_limit_bytes=VMEM_LIMIT),
        cost_estimate=pl.CostEstimate(
            flops=12 * count * count * depth,
            bytes_accessed=8 * count * depth,
            transcendentals=0,
        ),
        name="gram_chunk",
    )(*args)


def eliminate(rows, following, at):
    n, count = rows.shape
    sub = iota((n, LANES), 0)
    lane, sub_all = iota((n, count), 1), iota((n, count), 0)
    own = (lane >= at) & (lane < at + n)

    def spread(values):
        return [jnp.broadcast_to(values[:, at + k : at + k + 1], (n, LANES)) for k in range(n)]

    def cut(values):
        return [values[:, h : h + LANES] for h in range(0, count, LANES)]

    columns = spread(rows)
    halves = cut(jnp.where(own, jnp.where(lane - at == sub_all, 1.0, 0.0), rows))
    if following is not None:
        next_columns = spread(following)
        next_halves = cut(jnp.where(own, 0.0, following))
    pivots = jnp.ones((n, LANES), jnp.float32)
    inverses = jnp.zeros((n, LANES), jnp.float32)
    for k in range(n):
        pivot = columns[k][k : k + 1, :]
        inverse = 1.0 / pivot
        pivots = jnp.where(sub == k, jnp.broadcast_to(pivot, (n, LANES)), pivots)
        inverses = jnp.where(sub == k, jnp.broadcast_to(inverse, (n, LANES)), inverses)
        factor = jnp.where(sub > k, columns[k] * inverse, 0.0)
        if following is not None:
            next_factor = next_columns[k] * inverse
        for j in range(k + 1, n):
            row = columns[j][k : k + 1, :]
            columns[j] = columns[j] - factor * row
            if following is not None:
                next_columns[j] = next_columns[j] - next_factor * row
        for h, half in enumerate(halves):
            row = half[k : k + 1, :]
            halves[h] = half - factor * row
            if following is not None:
                next_halves[h] = next_halves[h] - next_factor * row
    upper = jnp.zeros((n, LANES), jnp.float32)
    lane_here = iota((n, LANES), 1) + at // LANES * LANES
    for k in range(n):
        upper = jnp.where(lane_here == at + k, columns[k], upper)
    carried = None if following is None else jnp.concatenate(next_halves, axis=1)
    return halves, upper, pivots, inverses, carried


def factorize(work, factor_ref, inverse_ref):
    count = work.shape[0]
    n = PANEL
    lane, sub = iota((n, LANES), 1), iota((n, LANES), 0)
    rows = work[:n, :]
    for at in range(0, count, n):
        below, later = at + n, at + 2 * n
        following = work[below:later, :] if below < count else None
        halves, upper, pivots, inverses, rows = eliminate(rows, following, at)
        root = lax.rsqrt(pivots)
        root = root * (1.5 - 0.5 * pivots * root * root)
        scaled = []
        for h, half in enumerate(halves):
            column = lane + h * LANES
            mixed = jnp.where((column >= at) & (column < below), upper, half)
            cut = slice(h * LANES, (h + 1) * LANES)
            factor_ref[at:below, cut] = jnp.where(column >= sub + at, mixed * root, 0.0)
            inverse_ref[at:below, cut] = jnp.where(column <= sub + at, half * root, 0.0)
            scaled.append(jnp.where(column >= later, half * inverses, 0.0))
        if later >= count:
            continue
        skip = later // LANES
        multiplier = jnp.concatenate([part.T for part in scaled[skip:]], axis=0)
        finished = jnp.concatenate(halves, axis=1)
        for top, end in ((later, later + n), (later + n, count)):
            if top >= end:
                continue
            from_row = skip * LANES
            update = dot(multiplier[top - from_row : end - from_row], finished, precision=HIGHEST)
            wide = iota((end - top, count), 1)
            old = jnp.where((wide >= at) & (wide < below), 0.0, work[top:end, :])
            work[top:end, :] = old - update


def finish_kernel(*refs, chunks, samples):
    own_ref, other_ref = refs[:2]
    highs, lows = refs[2 : 2 + chunks], refs[2 + chunks : 2 + 2 * chunks]
    basis_ref, *square_refs = refs[2 + 2 * chunks : 6 + 2 * chunks]
    pack_ref, work, inverse_ref, rows_ref, out_sem, *own_squares, square_sem = refs[
        6 + 2 * chunks :
    ]
    factor_ref, projected_ref, operator_ref = own_squares
    count = work.shape[0]
    half = count // 2

    scale = 1.0 / samples
    rows = own_ref.shape[0]
    core = jnp.bitwise_and(lax.axis_index("rows"), 1)
    pack_ref[pl.ds(pl.multiple_of(core * rows, 8), rows), :] = own_ref[...] * scale
    pack_ref[pl.ds(pl.multiple_of((1 - core) * rows, 8), rows), :] = other_ref[...] * scale
    mixed = pack_ref[:half, :]
    row, col = iota((half, half), 0), iota((half, half), 1)
    diagonal = pack_ref[2 * half : 2 * half + 1, :]
    turned = mixed.T
    work[:half, :half] = jnp.where(col >= row, mixed, turned)
    cross = pack_ref[half : 2 * half, :]
    work[:half, half:] = cross
    work[half:, :half] = cross.T
    work[half:, half:] = jnp.where(col > row, turned, jnp.where(col == row, diagonal, mixed))
    factorize(work, factor_ref, inverse_ref)

    inverse = inverse_ref[...]
    tail = [pack_ref[2 * half + r : 2 * half + r + 1, :] for r in (1, 2)]
    column = jnp.sum(inverse * jnp.concatenate(tail, axis=1), axis=1, keepdims=True)
    shifted = pltpu.roll(factor_ref[...], count - 1, 1)
    projected = jnp.where(iota((count, count), 1) == count - 1, column, shifted)
    projected_ref[...] = projected
    operator_ref[...] = dot(projected, inverse, dims=((1,), (1,)), precision=HIGHEST)
    stores = []
    for index, (source, target) in enumerate(zip(own_squares, square_refs)):
        copy = pltpu.make_async_copy(source, target, square_sem.at[index])
        copy.start()
        stores.append(copy)

    turned_high, turned_low = split(inverse.T)
    turned = jnp.concatenate([turned_high, turned_high, turned_low], axis=0)
    tiles = 0
    done = 0
    for high_ref, low_ref in zip(highs, lows):
        for at in range(0, high_ref.shape[0], BASIS_TILE):
            size = min(BASIS_TILE, high_ref.shape[0] - at)
            high, low = high_ref[at : at + size, :], low_ref[at : at + size, :]
            tile = pl.ds(done, size)
            rows_ref[tile, :] = dot(jnp.concatenate([high, low, high], axis=1), turned)
            copy = pltpu.make_async_copy(
                rows_ref.at[tile], basis_ref.at[tile], out_sem.at[tiles]
            )
            copy.start()
            stores.append(copy)
            tiles += 1
            done += size

    for copy in stores:
        copy.wait()


def finish(own, other, highs, lows, samples):
    chunks = len(highs)
    count = highs[0].shape[1]
    depth = sum(h.shape[0] for h in highs)
    tiles = sum(-(-h.shape[0] // BASIS_TILE) for h in highs)
    square = jax.ShapeDtypeStruct((count, count), jnp.float32)
    vmem = pl.BlockSpec(memory_space=pltpu.VMEM)
    far = pl.BlockSpec(memory_space=pl.ANY)
    return pl.pallas_call(
        functools.partial(finish_kernel, chunks=chunks, samples=samples),
        out_shape=(jax.ShapeDtypeStruct((depth, count), jnp.float32), square, square, square),
        in_specs=[vmem] * (2 + 2 * chunks),
        out_specs=(far,) * 4,
        scratch_shapes=[
            pltpu.VMEM((2 * own.shape[0], LANES), jnp.float32),
            pltpu.VMEM((count, count), jnp.float32),
            pltpu.VMEM((count, count), jnp.float32),
            pltpu.VMEM((depth, count), jnp.float32),
            pltpu.SemaphoreType.DMA((tiles,)),
            *[pltpu.VMEM((count, count), jnp.float32)] * 3,
            pltpu.SemaphoreType.DMA((3,)),
        ],
        compiler_params=pltpu.CompilerParams(vmem_limit_bytes=VMEM_LIMIT),
        name="factor_and_basis",
    )(own, other, *highs, *lows)


def swap(values, axis, step):
    size = lax.axis_size(axis)
    return lax.ppermute(values, axis, [(i, i ^ step) for i in range(size)])


def sum_halves(keep, send):
    keep = keep + swap(send, "rows", 1)
    for axis, step in (("rows", 2), ("tm", 1)):
        size = lax.axis_size(axis)
        while step < size:
            if 2 * step < size:
                far = swap(keep, axis, 3 * step)
                near = swap(keep, axis, step)
                other = swap(keep, axis, 2 * step)
                keep = (keep + near) + (other + far)
            else:
                keep = keep + swap(keep, axis, step)
            step *= 4
    return keep, swap(keep, "rows", 1)


def shards(snapshots, last_snapshot):
    peers = lax.axis_size("tm")
    devices = peers * lax.axis_size("rows")
    me = lax.axis_index("tm")
    own_cols = snapshots.shape[1]
    count = own_cols * peers
    depth = snapshots.shape[0] // peers
    columns = snapshots.T

    small = depth // 8
    first = depth // 6 // LANES * LANES
    large = (depth - small - first) // (4 * LANES) * (2 * LANES)
    sizes = [first, depth - small - first - large, large, small]

    def cut(values, offset, start, size):
        target = jnp.bitwise_xor(me, offset)
        return lax.dynamic_slice(values, (0, target * depth + start), (own_cols, size))

    far = range(2, peers)
    columns, *early = lax.optimization_barrier(
        (columns, *[cut(columns, offset, 0, first) for offset in far])
    )
    early = {offset: swap(piece, "tm", offset) for offset, piece in zip(far, early)}
    tail_own = jnp.dot(
        columns, last_snapshot, precision=HIGHEST, preferred_element_type=jnp.float32
    )
    columns, tail_own = lax.optimization_barrier((columns, tail_own))
    chunks = []
    start = 0
    for size in sizes:
        pieces = []
        for offset in range(peers):
            if start == 0 and offset in early:
                pieces.append(early[offset])
                continue
            piece = cut(columns, offset, start, size)
            pieces.append(swap(piece, "tm", offset) if offset else piece)
        chunks.append(pieces)
        start += size

    tail = lax.dynamic_update_slice_in_dim(
        jnp.zeros((count,), jnp.float32), tail_own, me * own_cols, 0
    ).reshape(count // LANES, LANES)

    running = None
    highs, lows = [], []
    for index, pieces in enumerate(chunks):
        ending = index == len(chunks) - 1
        *running, high, low = add_chunk(pieces, running, tail if ending else None)
        running = running if ending else running[0]
        highs.append(high)
        lows.append(low)
    own, other = sum_halves(*running)
    basis, factor, projected, operator = finish(own, other, highs, lows, depth * devices)
    return (basis.reshape(1, 1, depth, count), factor, projected, operator)


def solution(mesh):
    in_specs = (P("rows", "tm"), P("rows"))
    out_specs = (P("rows", "tm", None, None), P(), P(), P())
    return jax.shard_map(shards, mesh=mesh, in_specs=in_specs, out_specs=out_specs, check_vma=False)
```

```python
import functools

import jax
import jax.numpy as jnp
from jax import lax
from jax.experimental import pallas as pl
from jax.experimental.pallas import tpu as pltpu
from jax.sharding import PartitionSpec as P

HIGHEST = lax.Precision.HIGHEST
LANES = 128
PANEL = 16
BASIS_TILE = 256
VMEM_LIMIT = 24 * 1024 * 1024


def iota(shape, dim):
    return lax.broadcasted_iota(jnp.int32, shape, dim)


def split(values):
    first = values.astype(jnp.bfloat16)
    second = (values - first.astype(jnp.float32)).astype(jnp.bfloat16)
    return first, second


def dot(left, right, dims=((1,), (0,)), precision=None):
    return lax.dot_general(
        left, right, (dims, ((), ())), precision=precision, preferred_element_type=jnp.float32
    )


def widen(pieces, cols_ref):
    width = pieces[0].shape[0]
    me = lax.axis_index("tm")
    for offset, piece in enumerate(pieces):
        start = pl.multiple_of(jnp.bitwise_xor(me, offset) * width, width)
        cols_ref[pl.ds(start, width), :] = piece[...]


def gram_of(cols_ref, high_ref, low_ref):
    depth = cols_ref.shape[1]
    total = None
    step = 2 * LANES if depth % (2 * LANES) == 0 else LANES
    for at in range(0, depth, step):
        cols = cols_ref[:, at : at + step]
        rows = cols.T
        high, low = split(rows)
        high_ref[at : at + step, :] = high
        low_ref[at : at + step, :] = low
        part = dot(cols, rows, precision=HIGHEST)
        total = part if total is None else total + part
    half = total.shape[0] // 2
    return total[:half, :half], total[:half, half:], total[half:, half:]


def first_kernel(*refs, peers):
    out_ref, high_ref, low_ref, cols_ref = refs[peers:]
    widen(refs[:peers], cols_ref)
    for index, block in enumerate(gram_of(cols_ref, high_ref, low_ref)):
        out_ref[index] = block


def middle_kernel(*refs, peers):
    sum_ref, out_ref, high_ref, low_ref, cols_ref = refs[peers:]
    widen(refs[:peers], cols_ref)
    for index, block in enumerate(gram_of(cols_ref, high_ref, low_ref)):
        out_ref[index] = sum_ref[index] + block


def last_kernel(*refs, peers):
    sum_ref, tail_ref, keep_ref, send_ref, high_ref, low_ref, cols_ref, pack_ref = refs[peers:]
    widen(refs[:peers], cols_ref)
    first, cross, second = (
        sum_ref[index] + block
        for index, block in enumerate(gram_of(cols_ref, high_ref, low_ref))
    )
    size = first.shape[0]
    row, col = iota(first.shape, 0), iota(first.shape, 1)
    pack_ref[:size, :] = jnp.where(col >= row, first, second)
    pack_ref[size : 2 * size, :] = cross
    pack_ref[2 * size :, :] = jnp.zeros((pack_ref.shape[0] - 2 * size, LANES), jnp.float32)
    pack_ref[2 * size : 2 * size + 1, :] = jnp.sum(
        jnp.where(col == row, second, 0.0), axis=0, keepdims=True
    )
    pack_ref[2 * size + 1 : 2 * size + 3, :] = tail_ref[...]
    rows = keep_ref.shape[0]
    core = jnp.bitwise_and(lax.axis_index("rows"), 1)
    keep_ref[...] = pack_ref[pl.ds(pl.multiple_of(core * rows, 8), rows), :]
    send_ref[...] = pack_ref[pl.ds(pl.multiple_of((1 - core) * rows, 8), rows), :]


def add_chunk(pieces, running, tail):
    peers = len(pieces)
    width, depth = pieces[0].shape
    count = width * peers
    half = count // 2
    vmem = pl.BlockSpec(memory_space=pltpu.VMEM)
    terms = (jax.ShapeDtypeStruct((depth, count), jnp.bfloat16),) * 2
    scratch = [pltpu.VMEM((count, depth), jnp.float32)]
    if tail is None:
        sums = (jax.ShapeDtypeStruct((3, half, half), jnp.float32),)
        args = (*pieces,) if running is None else (*pieces, running)
        body = first_kernel if running is None else middle_kernel
    else:
        rows = (2 * half + 3 + 15) // 16 * 8
        sums = (jax.ShapeDtypeStruct((rows, LANES), jnp.float32),) * 2
        args = (*pieces, running, tail)
        body = last_kernel
        scratch.append(pltpu.VMEM((2 * rows, LANES), jnp.float32))
    return pl.pallas_call(
        functools.partial(body, peers=peers),
        out_shape=sums + terms,
        in_specs=[vmem] * len(args),
        out_specs=(vmem,) * (len(sums) + 2),
        scratch_shapes=scratch,
        compiler_params=pltpu.CompilerParams(vmem_limit_bytes=VMEM_LIMIT),
        cost_estimate=pl.CostEstimate(
            flops=12 * count * count * depth,
            bytes_accessed=8 * count * depth,
            transcendentals=0,
        ),
        name="gram_chunk",
    )(*args)


def eliminate(rows, following, at):
    n, count = rows.shape
    sub = iota((n, LANES), 0)
    lane, sub_all = iota((n, count), 1), iota((n, count), 0)
    own = (lane >= at) & (lane < at + n)

    def spread(values):
        return [jnp.broadcast_to(values[:, at + k : at + k + 1], (n, LANES)) for k in range(n)]

    def cut(values):
        return [values[:, h : h + LANES] for h in range(0, count, LANES)]

    columns = spread(rows)
    halves = cut(jnp.where(own, jnp.where(lane - at == sub_all, 1.0, 0.0), rows))
    if following is not None:
        next_columns = spread(following)
        next_halves = cut(jnp.where(own, 0.0, following))
    pivots = jnp.ones((n, LANES), jnp.float32)
    inverses = jnp.zeros((n, LANES), jnp.float32)
    for k in range(n):
        pivot = columns[k][k : k + 1, :]
        inverse = 1.0 / pivot
        pivots = jnp.where(sub == k, jnp.broadcast_to(pivot, (n, LANES)), pivots)
        inverses = jnp.where(sub == k, jnp.broadcast_to(inverse, (n, LANES)), inverses)
        factor = jnp.where(sub > k, columns[k] * inverse, 0.0)
        if following is not None:
            next_factor = next_columns[k] * inverse
        for j in range(k + 1, n):
            row = columns[j][k : k + 1, :]
            columns[j] = columns[j] - factor * row
            if following is not None:
                next_columns[j] = next_columns[j] - next_factor * row
        for h, half in enumerate(halves):
            row = half[k : k + 1, :]
            halves[h] = half - factor * row
            if following is not None:
                next_halves[h] = next_halves[h] - next_factor * row
    upper = jnp.zeros((n, LANES), jnp.float32)
    lane_here = iota((n, LANES), 1) + at // LANES * LANES
    for k in range(n):
        upper = jnp.where(lane_here == at + k, columns[k], upper)
    carried = None if following is None else jnp.concatenate(next_halves, axis=1)
    return halves, upper, pivots, inverses, carried


def factorize(work, factor_ref, inverse_ref):
    count = work.shape[0]
    n = PANEL
    lane, sub = iota((n, LANES), 1), iota((n, LANES), 0)
    rows = work[:n, :]
    for at in range(0, count, n):
        below, later = at + n, at + 2 * n
        following = work[below:later, :] if below < count else None
        halves, upper, pivots, inverses, rows = eliminate(rows, following, at)
        root = lax.rsqrt(pivots)
        root = root * (1.5 - 0.5 * pivots * root * root)
        scaled = []
        for h, half in enumerate(halves):
            column = lane + h * LANES
            mixed = jnp.where((column >= at) & (column < below), upper, half)
            cut = slice(h * LANES, (h + 1) * LANES)
            factor_ref[at:below, cut] = jnp.where(column >= sub + at, mixed * root, 0.0)
            inverse_ref[at:below, cut] = jnp.where(column <= sub + at, half * root, 0.0)
            scaled.append(jnp.where(column >= later, half * inverses, 0.0))
        if later >= count:
            continue
        skip = later // LANES
        multiplier = jnp.concatenate([part.T for part in scaled[skip:]], axis=0)
        finished = jnp.concatenate(halves, axis=1)
        for top, end in ((later, later + n), (later + n, count)):
            if top >= end:
                continue
            from_row = skip * LANES
            update = dot(multiplier[top - from_row : end - from_row], finished, precision=HIGHEST)
            wide = iota((end - top, count), 1)
            old = jnp.where((wide >= at) & (wide < below), 0.0, work[top:end, :])
            work[top:end, :] = old - update


def finish_kernel(*refs, chunks, samples):
    own_ref, other_ref = refs[:2]
    highs, lows = refs[2 : 2 + chunks], refs[2 + chunks : 2 + 2 * chunks]
    basis_ref, *square_refs = refs[2 + 2 * chunks : 6 + 2 * chunks]
    pack_ref, work, inverse_ref, rows_ref, out_sem, *own_squares, square_sem = refs[
        6 + 2 * chunks :
    ]
    factor_ref, projected_ref, operator_ref = own_squares
    count = work.shape[0]
    half = count // 2

    scale = 1.0 / samples
    rows = own_ref.shape[0]
    core = jnp.bitwise_and(lax.axis_index("rows"), 1)
    pack_ref[pl.ds(pl.multiple_of(core * rows, 8), rows), :] = own_ref[...] * scale
    pack_ref[pl.ds(pl.multiple_of((1 - core) * rows, 8), rows), :] = other_ref[...] * scale
    mixed = pack_ref[:half, :]
    row, col = iota((half, half), 0), iota((half, half), 1)
    diagonal = pack_ref[2 * half : 2 * half + 1, :]
    turned = mixed.T
    work[:half, :half] = jnp.where(col >= row, mixed, turned)
    cross = pack_ref[half : 2 * half, :]
    work[:half, half:] = cross
    work[half:, :half] = cross.T
    work[half:, half:] = jnp.where(col > row, turned, jnp.where(col == row, diagonal, mixed))
    factorize(work, factor_ref, inverse_ref)

    inverse = inverse_ref[...]
    stores = []
    turned_high, turned_low = split(inverse.T)
    turned = jnp.concatenate([turned_high, turned_high, turned_low], axis=0)
    tiles = 0
    done = 0
    for chunk, (high_ref, low_ref) in enumerate(zip(highs, lows)):
        if chunk == chunks - 1:
            tail = [pack_ref[2 * half + r : 2 * half + r + 1, :] for r in (1, 2)]
            column = jnp.sum(inverse * jnp.concatenate(tail, axis=1), axis=1, keepdims=True)
            shifted = pltpu.roll(factor_ref[...], count - 1, 1)
            projected = jnp.where(iota((count, count), 1) == count - 1, column, shifted)
            projected_ref[...] = projected
            operator_ref[...] = dot(projected, inverse, dims=((1,), (1,)), precision=HIGHEST)
            for index, (source, target) in enumerate(zip(own_squares, square_refs)):
                copy = pltpu.make_async_copy(source, target, square_sem.at[index])
                copy.start()
                stores.append(copy)
        for at in range(0, high_ref.shape[0], BASIS_TILE):
            size = min(BASIS_TILE, high_ref.shape[0] - at)
            high, low = high_ref[at : at + size, :], low_ref[at : at + size, :]
            tile = pl.ds(done, size)
            rows_ref[tile, :] = dot(jnp.concatenate([high, low, high], axis=1), turned)
            copy = pltpu.make_async_copy(
                rows_ref.at[tile], basis_ref.at[tile], out_sem.at[tiles]
            )
            copy.start()
            stores.append(copy)
            tiles += 1
            done += size

    for copy in stores:
        copy.wait()


def finish(own, other, highs, lows, samples):
    chunks = len(highs)
    count = highs[0].shape[1]
    depth = sum(h.shape[0] for h in highs)
    tiles = sum(-(-h.shape[0] // BASIS_TILE) for h in highs)
    square = jax.ShapeDtypeStruct((count, count), jnp.float32)
    vmem = pl.BlockSpec(memory_space=pltpu.VMEM)
    far = pl.BlockSpec(memory_space=pl.ANY)
    return pl.pallas_call(
        functools.partial(finish_kernel, chunks=chunks, samples=samples),
        out_shape=(jax.ShapeDtypeStruct((depth, count), jnp.float32), square, square, square),
        in_specs=[vmem] * (2 + 2 * chunks),
        out_specs=(far,) * 4,
        scratch_shapes=[
            pltpu.VMEM((2 * own.shape[0], LANES), jnp.float32),
            pltpu.VMEM((count, count), jnp.float32),
            pltpu.VMEM((count, count), jnp.float32),
            pltpu.VMEM((depth, count), jnp.float32),
            pltpu.SemaphoreType.DMA((tiles,)),
            *[pltpu.VMEM((count, count), jnp.float32)] * 3,
            pltpu.SemaphoreType.DMA((3,)),
        ],
        compiler_params=pltpu.CompilerParams(vmem_limit_bytes=VMEM_LIMIT),
        name="factor_and_basis",
    )(own, other, *highs, *lows)


def swap(values, axis, step):
    size = lax.axis_size(axis)
    return lax.ppermute(values, axis, [(i, i ^ step) for i in range(size)])


def sum_halves(keep, send):
    keep = keep + swap(send, "rows", 1)
    for axis, step in (("rows", 2), ("tm", 1)):
        size = lax.axis_size(axis)
        while step < size:
            if 2 * step < size:
                far = swap(keep, axis, 3 * step)
                near = swap(keep, axis, step)
                other = swap(keep, axis, 2 * step)
                keep = (keep + near) + (other + far)
            else:
                keep = keep + swap(keep, axis, step)
            step *= 4
    return keep, swap(keep, "rows", 1)


def shards(snapshots, last_snapshot):
    peers = lax.axis_size("tm")
    devices = peers * lax.axis_size("rows")
    me = lax.axis_index("tm")
    own_cols = snapshots.shape[1]
    count = own_cols * peers
    depth = snapshots.shape[0] // peers
    columns = snapshots.T

    small = depth // 8
    first = depth // 6 // LANES * LANES
    large = (depth - small - first) // (4 * LANES) * (2 * LANES)
    sizes = [first, depth - small - first - large, large, small]

    def cut(values, offset, start, size):
        target = jnp.bitwise_xor(me, offset)
        return lax.dynamic_slice(values, (0, target * depth + start), (own_cols, size))

    far = range(2, peers)
    columns, *early = lax.optimization_barrier(
        (columns, *[cut(columns, offset, 0, first) for offset in far])
    )
    early = {offset: swap(piece, "tm", offset) for offset, piece in zip(far, early)}
    tail_own = jnp.dot(
        columns, last_snapshot, precision=HIGHEST, preferred_element_type=jnp.float32
    )
    columns, tail_own = lax.optimization_barrier((columns, tail_own))
    chunks = []
    start = 0
    for size in sizes:
        pieces = []
        for offset in range(peers):
            if start == 0 and offset in early:
                pieces.append(early[offset])
                continue
            piece = cut(columns, offset, start, size)
            pieces.append(swap(piece, "tm", offset) if offset else piece)
        chunks.append(pieces)
        start += size

    tail = lax.dynamic_update_slice_in_dim(
        jnp.zeros((count,), jnp.float32), tail_own, me * own_cols, 0
    ).reshape(count // LANES, LANES)

    running = None
    highs, lows = [], []
    for index, pieces in enumerate(chunks):
        ending = index == len(chunks) - 1
        *running, high, low = add_chunk(pieces, running, tail if ending else None)
        running = running if ending else running[0]
        highs.append(high)
        lows.append(low)
    own, other = sum_halves(*running)
    basis, factor, projected, operator = finish(own, other, highs, lows, depth * devices)
    return (basis.reshape(1, 1, depth, count), factor, projected, operator)


def solution(mesh):
    in_specs = (P("rows", "tm"), P("rows"))
    out_specs = (P("rows", "tm", None, None), P(), P(), P())
    return jax.shard_map(shards, mesh=mesh, in_specs=in_specs, out_specs=out_specs, check_vma=False)
```
